32 devices in a mesh: lat: 2 (over x), lon: 8 (over z, y), grp: 2 (over core).
Axes of the slice: x: 2, y: 2, z: 4, core: 2. Of those that a mesh axis runs over, the one named last changes fastest.
Arguments:
- teacher_in: bfloat16 [2, 48, 96, 512], P('grp', 'lat', 'lon'), may hold values from -6 to 6
- student_in: bfloat16 [2, 48, 96, 256], P('grp', 'lat', 'lon'), may hold values from -6 to 6
- regions: int32 [2, 48, 96], P(None, 'lat', 'lon'), may hold values from 0 to 2
- t_qkv: bfloat16 [2, 512, 1536], replicated, may hold values from -0.25 to 0.25
- t_out: bfloat16 [2, 512, 512], replicated, may hold values from -0.25 to 0.25
- s_qkv: bfloat16 [2, 256, 768], replicated, may hold values from -0.375 to 0.375
- s_out: bfloat16 [2, 256, 256], replicated, may hold values from -0.375 to 0.375
- s_proj: bfloat16 [256, 512], replicated, may hold values from -0.375 to 0.375
Outputs:
- teacher_out: bfloat16 [2, 48, 96, 512], P('grp', 'lat', 'lon')
- student_grad: float32 [2, 48, 96, 256], P('grp', 'lat', 'lon')
The draws below stay inside these ranges and needn't reach their ends.
All inputs are finite; a program needn't handle non-finite values.
Results may differ from the reference program's by a relative error of at most 0.02.
Values may be sent and summed in bfloat16 or wider, within the bound.
A program may use at most 128 MiB of HBM per device.

```python
import jax
import jax.numpy as jnp
from jax import lax

D_T = 512
HEADS_T = 8
D_S = 256
HEADS_S = 4
LEV = 2
LAYERS = 2
LAT = 48
LON = 96


def place_ends(drawn, stream_key, smallest, top_value):
    spot = [jax.random.randint(jax.random.fold_in(stream_key, axis), (), 0, length) for axis, length in enumerate(drawn.shape)]
    main_axis = drawn.shape.index(max(drawn.shape))
    next_to = spot[:main_axis] + [(spot[main_axis] + 1) % drawn.shape[main_axis]] + spot[main_axis + 1:]
    return drawn.at[tuple(spot)].set(smallest).at[tuple(next_to)].set(top_value)


def level_of(stream_key, dims, cuts, low, largest):
    factor_of = 1.0
    for position, parts in cuts:
        steps = jax.random.uniform(jax.random.fold_in(jax.random.fold_in(stream_key, 6), position), (parts,), jnp.float32, low / len(cuts), largest / len(cuts))
        factor_of = factor_of * jnp.repeat(jnp.exp(steps), dims[position] // parts).reshape((-1,) + (1,) * (len(dims) - 1 - position))
    return factor_of


def centred(stream_key, dims, deviation, bound, pieces=(), kind=jnp.bfloat16):
    factor_of = level_of(stream_key, dims, pieces, -0.22, 0.18) if pieces else 1.0
    values = jax.random.normal(stream_key, dims, jnp.float32) * deviation * factor_of
    return jnp.minimum(jnp.maximum(values, -bound), bound).astype(kind)


def setup_inputs(seed: int = 0) -> dict:
    keys = jax.random.split(jax.random.key(seed), 9)
    return {
        "teacher_in": centred(keys[0], (LEV, LAT, LON, D_T), 1.0, 6.0, ((0, 2), (1, 2), (2, 8))),
        "student_in": centred(keys[1], (LEV, LAT, LON, D_S), 1.0, 6.0, ((0, 2), (1, 2), (2, 8))),
        "regions": place_ends(jax.random.randint(keys[2], (LEV, LAT, LON), 0, 3), jax.random.fold_in(keys[2], 1), 0, 2).astype(jnp.int32),
        "t_qkv": centred(keys[3], (LAYERS, D_T, 3 * D_T), D_T ** -0.5, 0.25),
        "t_out": centred(keys[4], (LAYERS, D_T, D_T), D_T ** -0.5, 0.25),
        "s_qkv": centred(keys[5], (LAYERS, D_S, 3 * D_S), D_S ** -0.5, 0.375),
        "s_out": centred(keys[6], (LAYERS, D_S, D_S), D_S ** -0.5, 0.375),
        "s_proj": centred(keys[7], (D_S, D_T), D_S ** -0.5, 0.375),
    }


logit_scale = 10.0
eps = 1e-06

def windows(source, win_rows, win_cols):
    levels, height, breadth = (source.shape[0], source.shape[1], source.shape[2])
    trailing = source.shape[3:]
    shaped = source.reshape((levels, height // win_rows, win_rows, breadth // win_cols, win_cols) + trailing)
    permute = (1, 3, 0, 2, 4) + tuple(range(5, 5 + len(trailing)))
    shaped = shaped.transpose(permute)
    return shaped.reshape((height // win_rows * (breadth // win_cols), levels * win_rows * win_cols) + trailing)

def unwindows(windowed, levels, height, breadth, win_rows, win_cols):
    trailing = windowed.shape[2:]
    shaped = windowed.reshape((height // win_rows, breadth // win_cols, levels, win_rows, win_cols) + trailing)
    permute = (2, 0, 3, 1, 4) + tuple(range(5, 5 + len(trailing)))
    return shaped.transpose(permute).reshape((levels, height, breadth) + trailing)

def attend(queries, key_rows, value_rows, reg_query, reg_key, head_count):
    nwin, nquery, channels = queries.shape
    nkey = key_rows.shape[1]
    head_size = channels // head_count
    q_heads = queries.reshape(nwin, nquery, head_count, head_size).astype(jnp.float32)
    k_heads = key_rows.reshape(nwin, nkey, head_count, head_size).astype(jnp.float32)
    v_heads = value_rows.reshape(nwin, nkey, head_count, head_size).astype(jnp.float32)
    products = jnp.einsum('wqhd,wkhd->whqk', q_heads, k_heads)
    query_sq = lax.optimization_barrier(jnp.sum(q_heads * q_heads, axis=3))
    key_sq = lax.optimization_barrier(jnp.sum(k_heads * k_heads, axis=3))
    scale_q = lax.rsqrt(query_sq + eps).transpose(0, 2, 1)[:, :, :, None]
    scale_k = lax.rsqrt(key_sq + eps).transpose(0, 2, 1)[:, :, None, :]
    scores = logit_scale * products * scale_q * scale_k
    allowed = reg_query[:, :, None] == reg_key[:, None, :]
    exponent = jnp.where(allowed[:, None], jnp.exp(scores), jnp.zeros((), jnp.float32))
    denominator = lax.optimization_barrier(jnp.sum(exponent, axis=3, keepdims=True))
    weights = (exponent / jnp.where(denominator > 0, denominator, jnp.ones((), jnp.float32))).astype(jnp.bfloat16)
    blended = jnp.einsum('whqk,wkhd->wqhd', weights.astype(jnp.float32), v_heads)
    return blended.astype(jnp.bfloat16).reshape(nwin, nquery, channels)

def project(source, matrix):
    channels = source.shape[-1]
    flat = source.reshape(-1, channels).astype(jnp.bfloat16)
    result = jnp.dot(flat, matrix, preferred_element_type=jnp.float32).astype(jnp.bfloat16)
    return result.reshape(source.shape[:-1] + (matrix.shape[1],))

def finish(source, attended, w_output):
    channels = source.shape[-1]
    output = jnp.dot(attended.reshape(-1, channels), w_output, preferred_element_type=jnp.float32)
    normed = output * lax.rsqrt(lax.optimization_barrier(jnp.mean(output * output, axis=-1, keepdims=True)) + eps)
    return (source.reshape(-1, channels).astype(jnp.float32) + normed).astype(jnp.bfloat16).reshape(source.shape)

def student_grad(student_in, reg_own, target, s_qkv, s_out, s_proj, head_count):
    levels, height, breadth, channels = student_in.shape
    reg_win = windows(reg_own.reshape(1, levels * height, breadth), 12, 6)

    def loss_fn(inputs):
        hidden = inputs
        for layer_idx in range(s_qkv.shape[0]):
            projected = project(hidden, s_qkv[layer_idx]).reshape(1, levels * height, breadth, 3 * channels)
            queries = windows(projected[..., :channels], 12, 6)
            key_rows = windows(projected[..., channels:2 * channels], 12, 6)
            value_rows = windows(projected[..., 2 * channels:], 12, 6)
            attended = attend(queries, key_rows, value_rows, reg_win, reg_win, head_count)
            attended = unwindows(attended, 1, levels * height, breadth, 12, 6).reshape(levels, height, breadth, channels)
            hidden = finish(hidden, attended, s_out[layer_idx])
        predicted = jnp.dot(hidden.reshape(-1, channels), s_proj, preferred_element_type=jnp.float32)
        residual = predicted - target.reshape(-1, target.shape[-1]).astype(jnp.float32)
        return 0.5 * jnp.sum(residual * residual)
    loss_value, pullback = jax.vjp(loss_fn, student_in.astype(jnp.float32))
    return pullback(jnp.ones((), jnp.float32))[0]

def place(source, filler):
    rolled = jnp.roll(source, 3, axis=2)
    widths = ((0, 0), (6, 6), (0, 0)) + ((0, 0),) * (source.ndim - 3)
    return jnp.pad(rolled, widths, constant_values=filler)

def reference(teacher_in, student_in, regions, t_qkv, t_out, s_qkv, s_out, s_proj):
    levels, height, breadth, channels = teacher_in.shape
    projected = project(teacher_in, t_qkv[0])
    queries = windows(projected[..., :channels], 12, 6)
    key_rows = windows(projected[..., channels:2 * channels], 12, 6)
    value_rows = windows(projected[..., 2 * channels:], 12, 6)
    reg_win = windows(regions, 12, 6)
    attended = attend(queries, key_rows, value_rows, reg_win, reg_win, HEADS_T)
    attended = unwindows(attended, levels, height, breadth, 12, 6)
    hidden_a = finish(teacher_in, attended, t_out[0])
    projected = project(hidden_a, t_qkv[1])
    tall = height + 12
    placed = place(projected, 0.0).reshape(1, levels * tall, breadth, 3 * channels)
    reg_placed = place(regions, -1).reshape(1, levels * tall, breadth)
    queries = windows(placed[..., :channels], 12, 6)
    key_rows = windows(placed[..., channels:2 * channels], 12, 6)
    value_rows = windows(placed[..., 2 * channels:], 12, 6)
    reg_win = windows(reg_placed, 12, 6)
    attended = attend(queries, key_rows, value_rows, reg_win, reg_win, HEADS_T)
    attended = unwindows(attended, 1, levels * tall, breadth, 12, 6).reshape(levels, tall, breadth, channels)
    attended = jnp.roll(attended[:, 6:6 + height], -3, axis=2)
    teacher_out = finish(hidden_a, attended, t_out[1])
    gradient = student_grad(student_in, regions, teacher_out, s_qkv, s_out, s_proj, HEADS_S)
    return (teacher_out, gradient)
```

```python
import functools

import jax
import jax.numpy as jnp
import numpy as np
from jax import lax
from jax.experimental import pallas as pl
from jax.experimental.pallas import tpu as pltpu
from jax.sharding import PartitionSpec as P

HEADS_T = 8
HEADS_S = 4
SCALE = 10.0
EPS = 1e-06
BF = jnp.bfloat16
F32 = jnp.float32
MESH = pl.DeviceIdType.MESH

ROWS, COLS, PADC = 24, 12, 16
TOK = ROWS * PADC
BAND = 12 * PADC
HALF = 6 * PADC
SIDE = 96
FEAT = 128
SEC_L, SEC_R, SEC_TL, SEC_BL, SEC_TR, SEC_BR = (
    (0, 80),
    (80, 80),
    (160, 32),
    (192, 32),
    (224, 32),
    (256, 32),
)
PACK = 288


def dot(a, b):
    return jnp.dot(a, b, preferred_element_type=F32)


def dot_nt(a, b):
    return lax.dot_general(a, b, (((1,), (1,)), ((), ())), preferred_element_type=F32)


def dot_tn(a, b):
    return lax.dot_general(a, b, (((0,), (0,)), ((), ())), preferred_element_type=F32)


def constants():
    gather = np.zeros((PACK, TOK), np.float32)

    def put(section, rows, cols):
        at = section[0]
        for row in rows:
            for col in cols:
                gather[at, row * PADC + col] = 1
                at += 1

    top, bottom = range(6), range(ROWS - 6, ROWS)
    first, last = range(3), range(COLS - 3, COLS)
    put(SEC_L, range(ROWS), last)
    put(SEC_R, range(ROWS), first)
    put(SEC_TL, bottom, last)
    put(SEC_BL, top, last)
    put(SEC_TR, bottom, first)
    put(SEC_BR, top, first)
    spread = np.zeros((PACK, PACK), np.float32)
    for band in range(3):
        for line in range(12):
            row = band * 12 + line - 6
            for side, (mid, above, below) in enumerate(
                ((SEC_L, SEC_TL, SEC_BL), (SEC_R, SEC_TR, SEC_BR))
            ):
                if row < 0:
                    source = above[0] + (row + 6) * 3
                elif row >= ROWS:
                    source = below[0] + (row - ROWS) * 3
                else:
                    source = mid[0] + row * 3
                for col in range(3):
                    spread[band * SIDE + side * 36 + line * 3 + col, source + col] = 1
    token_col = np.arange(BAND) % PADC
    win = token_col // 6
    same = (win[:, None] == win[None, :]).astype(np.float32)
    shifted = (token_col + 3) // 6
    side_win = np.full((SIDE,), 99)
    side_win[:36] = 0
    side_win[36:72] = 2
    keys = np.concatenate([shifted, side_win])
    same_shifted = (shifted[:, None] == keys[None, :]).astype(np.float32)
    heads = (np.arange(256)[:, None] // 64 == np.arange(256)[None, :] // 64).astype(np.float32)
    of_row = (np.arange(TOK)[:, None] // PADC == np.arange(128)[None, :]).astype(np.float32)
    of_col = (np.arange(TOK)[:, None] % PADC == np.arange(128)[None, :]).astype(np.float32)
    return (
        jnp.asarray(gather, BF),
        jnp.asarray(spread, BF),
        jnp.asarray(same, F32),
        jnp.asarray(same_shifted, F32),
        jnp.asarray(heads, BF),
        jnp.asarray(of_row, BF),
        jnp.asarray(of_col, F32),
    )


def inverse_norm(values, heads):
    square = (values * values).astype(BF)
    parts = [
        dot(square[:, at : at + 256], heads) for at in range(0, values.shape[1], 256)
    ]
    total = parts[0] if len(parts) == 1 else jnp.concatenate(parts, axis=1)
    return lax.rsqrt(total + EPS)


def pair_masks():
    lane = lax.broadcasted_iota(jnp.int32, (1, 128), 1)
    low = jnp.where(lane < 64, 1.0, 0.0).astype(F32)
    return low.astype(BF), (1.0 - low).astype(BF)


def attend_pair(q, k, v, bias):
    low, high = pair_masks()
    exp_e = jnp.exp(dot_nt(q, k * low) + bias).astype(BF)
    exp_o = jnp.exp(dot_nt(q, k * high) + bias).astype(BF)
    out_e = dot(exp_e, v * low + high)
    out_o = dot(exp_o, v * high + low)
    is_low = lax.broadcasted_iota(jnp.int32, out_e.shape, 1) < 64
    total = jnp.where(is_low, out_e, out_o)
    den = pltpu.roll(jnp.where(is_low, out_o, out_e), 64, 1)
    return (total / jnp.where(den > 0, den, 1.0)).astype(BF)


def attend_pair_back(q, k, v, grad, bias):
    masks = pair_masks()
    dq = dk = dv = None
    for mask in masks:
        k_own = k * mask
        exps = jnp.exp(dot_nt(k_own, q) + bias)
        den = jnp.sum(exps, axis=0, keepdims=True)
        weights = exps * (1.0 / jnp.where(den > 0, den, 1.0))
        d_weights = dot_nt(v * mask, grad)
        inner = jnp.sum(weights * d_weights, axis=0, keepdims=True)
        d_scores = (weights * (d_weights - inner)).astype(BF)
        q_part = dot_tn(d_scores, k_own)
        k_part = dot(d_scores, q * mask)
        v_part = dot(weights.astype(BF), grad * mask)
        dq = q_part if dq is None else dq + q_part
        dk = k_part if dk is None else dk + k_part
        dv = v_part if dv is None else dv + v_part
    return dq, dk, dv


def bias_of(f_query, f_key, same):
    return (dot_nt(f_query, f_key) * same - 1.0) * 1e30


def lanes(pair):
    return pl.ds(pl.multiple_of(pair * 128, 128), 128)


def band_rows(band, size=BAND):
    return pl.ds(pl.multiple_of(band * size, 16), size)


def normed(o):
    return lax.rsqrt(jnp.mean(o * o, axis=-1, keepdims=True) + EPS)


def kernel(
    n_lat,
    n_lon,
    x_ref,
    s_ref,
    reg_ref,
    tqkv,
    tout,
    sqkv,
    sout,
    sproj,
    gather,
    spread,
    same,
    same_shifted,
    heads,
    of_row,
    of_col,
    out_ref,
    grad_ref,
    pad_t,
    pad_s,
    reg_pad,
    xa,
    qa,
    ka,
    va,
    bias_a,
    bias_s,
    bias_b,
    att,
    hext,
    pack,
    side_in,
    side,
    kb,
    vb,
    hid,
    q_s,
    k_s,
    v_s,
    rq_s,
    rk_s,
    o_s,
    att_s,
    pred,
    da_s,
    dqkv,
    send,
    recv,
):
    lat, lon, grp = lax.axis_index("lat"), lax.axis_index("lon"), lax.axis_index("grp")
    right, left = lax.rem(lon + 1, n_lon), lax.rem(lon + n_lon - 1, n_lon)
    has_up, has_down = lat > 0, lat < n_lat - 1
    barrier = pltpu.get_barrier_semaphore()

    def greet(device):
        pl.semaphore_signal(barrier, inc=1, device_id=device, device_id_type=MESH)

    greet((lat, lon, 1 - grp))
    greet((lat, left, grp))
    greet((lat, right, grp))

    @pl.when(has_up)
    def _():
        for column in (left, lon, right):
            greet((lat - 1, column, grp))

    @pl.when(has_down)
    def _():
        for column in (left, lon, right):
            greet((lat + 1, column, grp))

    pad_t[...] = jnp.zeros_like(pad_t)
    pad_t[:, 0:COLS, :] = x_ref[...]
    pad_s[...] = jnp.zeros_like(pad_s)
    pad_s[:, 0:COLS, :] = s_ref[...]
    reg_pad[...] = jnp.zeros_like(reg_pad)
    reg_pad[0:ROWS, 0:COLS] = (reg_ref[grp] + 1).astype(F32)
    region = jnp.sum(
        dot(of_row[...], reg_pad[...].astype(BF)) * of_col[...], axis=1, keepdims=True
    )
    lane = lax.broadcasted_iota(jnp.int32, (TOK, FEAT), 1).astype(F32)
    feature = jnp.where((region == lane) & (region > 0.5), 1.0, 0.0).astype(BF)
    xa[0:TOK, 0:512] = pad_t[...].reshape(TOK, 512)
    xa[0:TOK, 512:640] = feature
    hext[HALF : HALF + TOK, 512:640] = feature
    hid[0] = pad_s[...].reshape(TOK, 256)

    @pl.when(jnp.logical_not(has_up))
    def _():
        hext[0:HALF, :] = jnp.zeros((HALF, 640), BF)
        for at, size in (SEC_TL, SEC_TR):
            side_in[at : at + size, :] = jnp.zeros((size, 640), BF)

    @pl.when(jnp.logical_not(has_down))
    def _():
        hext[HALF + TOK :, :] = jnp.zeros((HALF, 640), BF)
        for at, size in (SEC_BL, SEC_BR):
            side_in[at : at + size, :] = jnp.zeros((size, 640), BF)

    rows_near = has_up.astype(jnp.int32) + has_down.astype(jnp.int32)
    pl.semaphore_wait(barrier, 3 + 3 * rows_near)

    def copy_to(source, target, slot, device):
        return pltpu.make_async_remote_copy(
            src_ref=source,
            dst_ref=target,
            send_sem=send.at[slot],
            recv_sem=recv.at[slot],
            device_id=device,
            device_id_type=MESH,
        )

    to_partner = copy_to(xa.at[0:TOK], xa.at[TOK : 2 * TOK], 0, (lat, lon, 1 - grp))
    to_partner.start()

    w_a = tqkv.at[0]

    def project_keys(rows, source, weight, k_ref, v_ref, target):
        value = source[rows, 0:512]
        keys = dot(value, weight[:, 512:1024]).astype(BF).astype(F32)
        k_ref[target, :] = (keys * inverse_norm(keys, heads[...])).astype(BF)
        v_ref[target, :] = dot(value, weight[:, 1024:1536]).astype(BF)

    def project_queries(value, weight):
        q = dot(value, weight[:, 0:512]).astype(BF).astype(F32)
        return (q * (inverse_norm(q, heads[...]) * SCALE)).astype(BF)

    def own_a(band, carry):
        rows = band_rows(band)
        qa[rows, :] = project_queries(xa[rows, 0:512], w_a)
        project_keys(rows, xa, w_a, ka, va, rows)
        own = xa[rows, 512:640]
        bias = bias_of(own, own, same[...])
        bias_s[rows, :] = bias
        return carry

    lax.fori_loop(0, 2, own_a, 0)
    to_partner.wait()

    def far_a(band, carry):
        rows = band_rows(band + 2)
        project_keys(rows, xa, w_a, ka, va, rows)
        return carry

    lax.fori_loop(0, 2, far_a, 0)

    def attend_a(band, carry):
        rows, far = band_rows(band), band_rows(band + 2)
        bias_a[:, 0:BAND] = bias_s[rows, :]
        bias_a[:, BAND : 2 * BAND] = bias_of(xa[rows, 512:640], xa[far, 512:640], same[...])

        def pair_a(pair, inner):
            cut = lanes(pair)
            att[rows, cut] = attend_pair(
                qa[rows, cut],
                jnp.concatenate([ka[rows, cut], ka[far, cut]], axis=0),
                jnp.concatenate([va[rows, cut], va[far, cut]], axis=0),
                bias_a[...],
            )
            return inner

        lax.fori_loop(0, 4, pair_a, 0)
        o = dot(att[rows, :], tout[0])
        hidden = (xa[rows, 0:512].astype(F32) + o * normed(o)).astype(BF)
        hext[pl.ds(pl.multiple_of(band * BAND + HALF, 16), BAND), 0:512] = hidden
        return carry

    lax.fori_loop(0, 2, attend_a, 0)

    pack[...] = dot(gather[...], hext[HALF : HALF + TOK, :]).astype(BF)

    def section(sec, slot, device):
        piece = pl.ds(sec[0], sec[1])
        return copy_to(pack.at[piece], side_in.at[piece], slot, device)

    to_right = section(SEC_L, 1, (lat, right, grp))
    to_left = section(SEC_R, 2, (lat, left, grp))
    ups = (
        copy_to(
            hext.at[HALF : 2 * HALF],
            hext.at[HALF + TOK : 2 * HALF + TOK],
            3,
            (lat - 1, lon, grp),
        ),
        section(SEC_BL, 4, (lat - 1, right, grp)),
        section(SEC_BR, 5, (lat - 1, left, grp)),
    )
    downs = (
        copy_to(hext.at[TOK : TOK + HALF], hext.at[0:HALF], 6, (lat + 1, lon, grp)),
        section(SEC_TL, 7, (lat + 1, right, grp)),
        section(SEC_TR, 8, (lat + 1, left, grp)),
    )
    to_right.start()
    to_left.start()

    @pl.when(has_up)
    def _():
        for copy in ups:
            copy.start()

    @pl.when(has_down)
    def _():
        for copy in downs:
            copy.start()

    for layer in range(2):

        def forward(band, carry, layer=layer):
            rows = band_rows(band)
            source = hid[layer, rows, :]
            w = sqkv.at[layer]
            q = dot(source, w[:, 0:256]).astype(BF).astype(F32)
            rq = inverse_norm(q, heads[...])
            rq_s[layer, rows, :] = rq
            q_s[layer, rows, :] = (q * (rq * SCALE)).astype(BF)
            k = dot(source, w[:, 256:512]).astype(BF).astype(F32)
            rk = inverse_norm(k, heads[...])
            rk_s[layer, rows, :] = rk
            k_s[layer, rows, :] = (k * rk).astype(BF)
            v_s[layer, rows, :] = dot(source, w[:, 512:768]).astype(BF)
            bias = bias_s[rows, :]
            for pair in range(2):
                cut = slice(pair * 128, pair * 128 + 128)
                att_s[rows, cut] = attend_pair(
                    q_s[layer, rows, cut], k_s[layer, rows, cut], v_s[layer, rows, cut], bias
                )
            o = dot(att_s[rows, :], sout[layer])
            o_s[layer, rows, :] = o
            hidden = (source.astype(F32) + o * normed(o)).astype(BF)
            if layer == 0:
                hid[1, rows, :] = hidden
            else:
                pred[rows, :] = dot(hidden, sproj[...])
            return carry

        lax.fori_loop(0, 2, forward, 0)

    w_b = tqkv.at[1]

    def own_b(band, carry):
        rows = pl.ds(pl.multiple_of(band * BAND + HALF, 16), BAND)
        qa[band_rows(band), :] = project_queries(hext[rows, 0:512], w_b)
        project_keys(rows, hext, w_b, kb, vb, rows)
        return carry

    lax.fori_loop(0, 2, own_b, 0)
    to_right.wait()
    to_left.wait()

    @pl.when(has_up)
    def _():
        for copy in ups:
            copy.wait_send()
        for copy in downs:
            copy.wait_recv()

    @pl.when(has_down)
    def _():
        for copy in downs:
            copy.wait_send()
        for copy in ups:
            copy.wait_recv()

    side[...] = dot(spread[...], side_in[...]).astype(BF)
    for start in (0, HALF + TOK):
        rows = slice(start, start + HALF)
        project_keys(rows, hext, w_b, kb, vb, rows)

    def side_b(band, carry):
        rows = band_rows(band, SIDE)
        target = pl.ds(pl.multiple_of(band * SIDE + 3 * BAND, 16), SIDE)
        project_keys(rows, side, w_b, kb, vb, target)
        return carry

    lax.fori_loop(0, 3, side_b, 0)

    spans = ((HALF, HALF), (2 * HALF, BAND), (4 * HALF, HALF))
    at = 0
    for band, (start, size) in enumerate(spans):
        f_key = jnp.concatenate(
            [
                hext[band * BAND : (band + 1) * BAND, 512:640],
                side[band * SIDE : (band + 1) * SIDE, 512:640],
            ],
            axis=0,
        )
        bias_b[at : at + size, :] = bias_of(
            hext[start : start + size, 512:640], f_key, same_shifted[0:size, :]
        )
        at += size

    def pair_b(pair, carry):
        cut = lanes(pair)
        done = 0
        for band, (start, size) in enumerate(spans):
            mid = slice(band * BAND, (band + 1) * BAND)
            edge = slice(3 * BAND + band * SIDE, 3 * BAND + (band + 1) * SIDE)
            att[done : done + size, cut] = attend_pair(
                qa[done : done + size, cut],
                jnp.concatenate([kb[mid, cut], kb[edge, cut]], axis=0),
                jnp.concatenate([vb[mid, cut], vb[edge, cut]], axis=0),
                bias_b[done : done + size, :],
            )
            done += size
        return carry

    lax.fori_loop(0, 4, pair_b, 0)

    def finish_b(band, carry):
        rows = band_rows(band)
        o = dot(att[rows, :], tout[1])
        source = hext[pl.ds(pl.multiple_of(band * BAND + HALF, 16), BAND), 0:512]
        result = (source.astype(F32) + o * normed(o)).astype(BF)
        block = pl.ds(band * 12, 12)
        out_ref[block, :, :] = result.reshape(12, PADC, 512)[:, 0:COLS, :]
        residual = pred[rows, :] - result.astype(F32)
        g = dot_nt(residual.astype(BF), sproj[...]).astype(BF).astype(F32)
        bias = bias_s[rows, :]
        for layer in (1, 0):
            o = o_s[layer, rows, :]
            scale = normed(o)
            y = o * scale
            d_o = scale * (g - y * jnp.mean(g * y, axis=-1, keepdims=True))
            da_s[rows, :] = dot_nt(d_o.astype(BF), sout[layer]).astype(BF)
            for pair in range(2):
                cut = slice(pair * 128, pair * 128 + 128)
                dq, dk, dv = attend_pair_back(
                    q_s[layer, rows, cut],
                    k_s[layer, rows, cut],
                    v_s[layer, rows, cut],
                    da_s[rows, cut],
                    bias,
                )
                for piece, value in enumerate((dq, dk, dv)):
                    first = piece * 256 + pair * 128
                    dqkv[rows, first : first + 128] = value
            dq = dqkv[rows, 0:256] * SCALE
            q_hat = q_s[layer, rows, :].astype(F32) * (1.0 / SCALE)
            along = dot((q_hat * dq).astype(BF), heads[...])
            dq = (rq_s[layer, rows, :] * (dq - q_hat * along)).astype(BF)
            dk = dqkv[rows, 256:512]
            k_hat = k_s[layer, rows, :].astype(F32)
            along = dot((k_hat * dk).astype(BF), heads[...])
            dk = (rk_s[layer, rows, :] * (dk - k_hat * along)).astype(BF)
            dv = dqkv[rows, 512:768].astype(BF)
            w = sqkv.at[layer]
            back = (
                dot_nt(dq, w[:, 0:256]) + dot_nt(dk, w[:, 256:512]) + dot_nt(dv, w[:, 512:768])
            )
            g = g + back
            if layer == 1:
                g = g.astype(BF).astype(F32)
        grad_ref[block, :, :] = g.reshape(12, PADC, 256)[:, 0:COLS, :]
        return carry

    lax.fori_loop(0, 2, finish_b, 0)


def solution(mesh):
    n_lat, n_lon = mesh.shape["lat"], mesh.shape["lon"]

    def shards(teacher_in, student_in, regions, t_qkv, t_out, s_qkv, s_out, s_proj):
        assert teacher_in.shape == (1, ROWS, COLS, 512)
        vm = pl.BlockSpec(memory_space=pltpu.VMEM)
        scratch = [
            ((ROWS, PADC, 512), BF),
            ((ROWS, PADC, 256), BF),
            ((128, 128), F32),
            ((2 * TOK, 640), BF),
            ((TOK, 512), BF),
            ((2 * TOK, 512), BF),
            ((2 * TOK, 512), BF),
            ((BAND, 2 * BAND), F32),
            ((TOK, BAND), F32),
            ((TOK, BAND + SIDE), F32),
            ((TOK, 512), BF),
            ((TOK + 2 * HALF, 640), BF),
            ((PACK, 640), BF),
            ((PACK, 640), BF),
            ((PACK, 640), BF),
            ((3 * BAND + 3 * SIDE, 512), BF),
            ((3 * BAND + 3 * SIDE, 512), BF),
            ((2, TOK, 256), BF),
            ((2, TOK, 256), BF),
            ((2, TOK, 256), BF),
            ((2, TOK, 256), BF),
            ((2, TOK, 256), F32),
            ((2, TOK, 256), F32),
            ((2, TOK, 256), F32),
            ((TOK, 256), BF),
            ((TOK, 512), F32),
            ((TOK, 256), BF),
            ((TOK, 768), F32),
        ]
        operands = (
            teacher_in[0],
            student_in[0],
            regions,
            t_qkv,
            t_out,
            s_qkv,
            s_out,
            s_proj,
        ) + constants()
        teacher_out, grad = pl.pallas_call(
            functools.partial(kernel, n_lat, n_lon),
            out_shape=(
                jax.ShapeDtypeStruct((ROWS, COLS, 512), BF),
                jax.ShapeDtypeStruct((ROWS, COLS, 256), F32),
            ),
            in_specs=[vm] * len(operands),
            out_specs=(vm, vm),
            scratch_shapes=[pltpu.VMEM(shape, kind) for shape, kind in scratch]
            + [pltpu.SemaphoreType.DMA((9,)), pltpu.SemaphoreType.DMA((9,))],
            compiler_params=pltpu.CompilerParams(
                collective_id=0, has_side_effects=True, vmem_limit_bytes=60 * 1024 * 1024
            ),
        )(*operands)
        return teacher_out[None], grad[None]

    return jax.shard_map(
        shards,
        mesh=mesh,
        in_specs=(
            P("grp", "lat", "lon", None),
            P("grp", "lat", "lon", None),
            P(None, "lat", "lon"),
            P(),
            P(),
            P(),
            P(),
            P(),
        ),
        out_specs=(P("grp", "lat", "lon", None), P("grp", "lat", "lon", None)),
        check_vma=False,
    )
```
